32 devices in a mesh: seq: 4 (over z), wsh: 8 (over y, x, core).
Axes of the slice: x: 2, y: 2, z: 4, core: 2. Of those that a mesh axis runs over, the one named last changes fastest.
Arguments:
- inputs: bfloat16 [8, 1024, 2048], P('wsh', 'seq'), may hold values from -6 to 6
- cotangent: bfloat16 [8, 1024, 2048], P('wsh', 'seq'), may hold values from -6 to 6
- teacher: bfloat16 [8, 1024, 2048], P('wsh', 'seq'), may hold values from -6 to 6
- document_ids: int32 [8, 1024], P('wsh'), may hold values from 0 to 9, never falling along the last dimension, each value on 1 to 512 neighbouring positions
- valid_flags: int32 [8, 1024], P('wsh', 'seq'), may hold values from 0 to 1, as said below
- step_count: int32 [1], replicated, may hold values from 1 to 20
- attn_params: float32 [2048, 8197], P(('seq', 'wsh')), may hold values from -2 to 2
- attn_first: float32 [2048, 8197], P(('seq', 'wsh')), may hold values from -8192 to 8192
- attn_second: float32 [2048, 8197], P(('seq', 'wsh')), may hold values from 0 to 49152, as said below
- mlp_params: float32 [2048, 16391], P(('seq', 'wsh')), may hold values from -2 to 2
- mlp_first: float32 [2048, 16391], P(('seq', 'wsh')), may hold values from -8192 to 8192
- mlp_second: float32 [2048, 16391], P(('seq', 'wsh')), may hold values from 0 to 49152, as said below
Outputs:
- block_output: bfloat16 [8, 1024, 2048], P('wsh', 'seq')
- losses: float32 [1], replicated
- input_grad: float32 [8, 1024, 2048], P('wsh', 'seq')
- vector_gradient: float32 [2048, 12], P(('seq', 'wsh'))
- attn_params_new: float32 [2048, 8197], P(('seq', 'wsh'))
- attn_first_new: float32 [2048, 8197], P(('seq', 'wsh'))
- attn_second_new: float32 [2048, 8197], P(('seq', 'wsh'))
- mlp_params_new: float32 [2048, 16391], P(('seq', 'wsh'))
- mlp_first_new: float32 [2048, 16391], P(('seq', 'wsh'))
- mlp_second_new: float32 [2048, 16391], P(('seq', 'wsh'))
The draws below stay inside these ranges and needn't reach their ends.
Inputs may be any that keep to these rules, and one draw needn't show every extreme that they name: `document_ids`: document numbers never fall along a sequence; a document has 1 to 512 tokens, and some document has exactly 512. `valid_flags`: in each sequence the valid tokens form a prefix of at least 256 tokens. `attn_second`: every entry is positive. `mlp_second`: every entry is positive.
All inputs are finite; a program needn't handle non-finite values.
Results may differ from the reference program's by a relative error of at most 0.007.
The reference program's roundings to bfloat16 on the way count: a program that leaves them out, or rounds other values in their place, can miss the bound.
Values may be sent and summed in bfloat16 or wider, within the bound.
A program may use at most 640 MiB of HBM per device.

```python
import math
import jax
import jax.numpy as jnp
import numpy as np
from jax import lax

D = 2048
H = 16
DH = 128
FF = 8192
QBLK = 512
SEQ = 1024
BATCH = 8
TOKENS = 8192
UPC = 4
ACOLS = 8197
MCOLS = 16391


def draw_valid_flags(key, part):
    jitter = jax.random.randint(key, (BATCH,), 0, SEQ // 8 + 1)
    ramp = 3 * (SEQ // 4) * jnp.arange(BATCH, dtype=jnp.int32) // max(BATCH - 1, 1)
    length = jnp.minimum(SEQ // 4 + ramp + jitter, SEQ)
    position = jnp.arange(SEQ, dtype=jnp.int32)
    return (position[None, :] < length[:, None]).astype(jnp.int32)


def attn_gradient_scale():
    columns = jnp.arange(ACOLS, dtype=jnp.int32)
    factor = jnp.where(columns < 3 * D, 3.0, jnp.where(columns < 4 * D, 1.1, jnp.where(columns < 4 * D + 2, 5.0, jnp.where(columns < 4 * D + 4, 3.0, 2.7))))
    return factor * math.sqrt(TOKENS)


def mlp_gradient_scale():
    columns = jnp.arange(MCOLS, dtype=jnp.int32)
    ratio = math.sqrt(D / FF)
    factor = jnp.where(columns < FF, 1.5 * ratio, jnp.where(columns < 2 * FF, 1.8, jnp.where(columns < 2 * FF + 2, 1.5, jnp.where(columns < 2 * FF + 2 + UPC, 1.5 * ratio, 2.5))))
    return factor * math.sqrt(TOKENS)


def first_moment(key, scale, width):
    key_size, key_sign = jax.random.split(key)
    size_draw = jax.random.uniform(key_size, (D, width), jnp.float32, 0.5, 1.5)
    sign_draw = (2 * jax.random.randint(key_sign, (D, width), 0, 2) - 1).astype(jnp.float32)
    return 0.1 / 0.9 * scale[None, :] * size_draw * sign_draw


def second_moment(key, scale, width):
    spread = jnp.exp(jax.random.uniform(key, (D, width), jnp.float32, math.log(0.5), math.log(2.0)))
    return 0.05 / 0.95 * 2.0 * scale[None, :] * scale[None, :] * spread


def draw_attn_params(key, part):
    key_normal, key_gain = jax.random.split(key)
    columns = jnp.arange(ACOLS, dtype=jnp.int32)[None, :]
    normal_draw = jax.random.normal(key_normal, (D, ACOLS), jnp.float32)
    gain_draw = jax.random.uniform(key_gain, (D, ACOLS), jnp.float32, 0.5, 1.5)
    spread = jnp.where(columns < 3 * D, 1.0 / math.sqrt(D), jnp.where(columns < 4 * D, 3.0 / math.sqrt(D), 0.3))
    return jnp.clip(jnp.where(columns == 4 * D, gain_draw, normal_draw * spread), -2.0, 2.0)


def draw_mlp_params(key, part):
    key_normal, key_gain = jax.random.split(key)
    columns = jnp.arange(MCOLS, dtype=jnp.int32)[None, :]
    normal_draw = jax.random.normal(key_normal, (D, MCOLS), jnp.float32)
    gain_draw = jax.random.uniform(key_gain, (D, MCOLS), jnp.float32, 0.5, 1.5)
    spread = jnp.where(columns < FF, 1.0 / math.sqrt(D), jnp.where(columns < 2 * FF, 1.0 / math.sqrt(FF), 0.3))
    return jnp.clip(jnp.where(columns == 2 * FF, gain_draw, normal_draw * spread), -2.0, 2.0)


def draw_attn_first(key, part):
    return first_moment(key, attn_gradient_scale(), ACOLS)


def draw_attn_second(key, part):
    return second_moment(key, attn_gradient_scale(), ACOLS)


def draw_mlp_first(key, part):
    return first_moment(key, mlp_gradient_scale(), MCOLS)


def draw_mlp_second(key, part):
    return second_moment(key, mlp_gradient_scale(), MCOLS)


def block_levels(rng, shape, pieces, smallest, largest):
    def one(dim, shards_of):
        steps = jax.random.uniform(jax.random.fold_in(jax.random.fold_in(rng, 6), dim), (shards_of,), jnp.float32, smallest / len(pieces), largest / len(pieces))
        return jnp.repeat(jnp.exp(steps), shape[dim] // shards_of).reshape((-1,) + (1,) * (len(shape) - dim - 1))

    level = one(*pieces[0])
    for cut in pieces[1:]:
        level = level * one(*cut)
    return level


def profile(number_of, total, reach, skew):
    portions = [(1 << 20) // math.isqrt(standing ** skew) + 1 for standing in range(2, number_of + 1)]
    rest, counts = total - reach - (number_of - 1), [1] * (number_of - 1)
    while rest > 0:
        movable = [i for i in range(number_of - 1) if counts[i] < reach]
        pool, left = sum([portions[i] for i in movable]), rest
        for i in movable:
            more = min(reach - counts[i], max(1, left * portions[i] // pool), rest)
            counts[i] = counts[i] + more
            rest = rest - more
    return np.array([reach] + counts)


def uneven(stream_key, count, total, limit, lean):
    if count == 2:
        one = jax.random.randint(stream_key, (), max(1, total - limit), min(limit, total - 1) + 1)
        return jnp.stack([one, total - one])
    tallies = jnp.asarray(profile(count, total, limit, lean), jnp.int32)
    couples = (count - 1) // 2
    donor, taker = tallies[1:1 + 2 * couples:2], tallies[2:2 + 2 * couples:2]
    margin = jnp.minimum(donor - 1, limit - taker)
    moved = jax.random.randint(jax.random.fold_in(stream_key, 1), (couples,), 0, 1 << 20) % (margin + 1)
    tallies = tallies.at[1:1 + 2 * couples:2].set(donor - moved).at[2:2 + 2 * couples:2].set(taker + moved)
    return tallies[jax.random.permutation(jax.random.fold_in(stream_key, 2), count)]


def scatter_about(key, dims, scale, bound, pieces=(), held_as=jnp.bfloat16):
    values = jax.random.normal(key, dims, jnp.float32) * scale
    if len(pieces) > 0:
        values = block_levels(key, dims, pieces, -0.22, 0.18) * values
    return jnp.clip(values, min=-bound, max=bound).astype(held_as)


def setup_inputs(seed: int = 0) -> dict:
    keys = jax.random.split(jax.random.key(seed), 13)
    inputs = scatter_about(keys[0], (BATCH, SEQ, D), 1.0, 6.0, ((0, 8), (1, 4)))
    cotangent = scatter_about(keys[1], (BATCH, SEQ, D), 1.0, 6.0, ((0, 8), (1, 4)))
    teacher = scatter_about(keys[2], (BATCH, SEQ, D), 1.0, 6.0, ((0, 8), (1, 4)))
    document_ids = jax.vmap(lambda own: jnp.searchsorted(jnp.cumsum(uneven(own, SEQ // 128 + 2, SEQ, SEQ // 2, 1)), jnp.arange(SEQ), side="right"))(jax.random.split(keys[3], BATCH)).reshape((BATCH, SEQ)).astype(jnp.int32)
    valid_flags = draw_valid_flags(jax.random.fold_in(keys[12], 71), 0)
    step_count = jax.random.randint(keys[5], (1,), 1, 21).astype(jnp.int32)
    attn_params = draw_attn_params(jax.random.fold_in(keys[12], 71), 0)
    attn_first = draw_attn_first(jax.random.fold_in(keys[12], 71), 0)
    attn_second = draw_attn_second(jax.random.fold_in(keys[12], 71), 0)
    mlp_params = draw_mlp_params(jax.random.fold_in(keys[12], 71), 0)
    mlp_first = draw_mlp_first(jax.random.fold_in(keys[12], 71), 0)
    mlp_second = draw_mlp_second(jax.random.fold_in(keys[12], 71), 0)
    return {"inputs": inputs, "cotangent": cotangent, "teacher": teacher, "document_ids": document_ids, "valid_flags": valid_flags, "step_count": step_count, "attn_params": attn_params, "attn_first": attn_first, "attn_second": attn_second, "mlp_params": mlp_params, "mlp_first": mlp_first, "mlp_second": mlp_second}


@jax.custom_vjp
def low(v):
    return lax.optimization_barrier(v.astype(jnp.bfloat16)).astype(jnp.float32)

@jax.custom_vjp
def low_back(v):
    return v

def low_keep(v):
    return (low(v), None)

def low_pass(kept, grad):
    return (grad,)

def back_keep(v):
    return (v, None)

def back_low(kept, grad):
    return (low(grad),)
low.defvjp(low_keep, low_pass)
low_back.defvjp(back_keep, back_low)
highest = lax.Precision.HIGHEST
eps_norm = 1e-05
beta_one = 0.9
beta_two = 0.95
adam_eps = 1e-08
decay_rate = 0.1
learn_rate = 0.05
gelu_coef = 0.7978845608028654

def layer_norm(value, gain, shift):
    row_mean = lax.optimization_barrier(jnp.mean(value, axis=-1, keepdims=True))
    centred = value - row_mean
    variance = lax.optimization_barrier(jnp.mean(centred * centred, axis=-1, keepdims=True))
    return centred * lax.rsqrt(variance + eps_norm) * gain + shift

def gelu_tanh(value):
    return 0.5 * value * (1.0 + jnp.tanh(gelu_coef * (value + 0.044715 * value * value * value)))

def attend(queries, keys_all, values, doc_row):
    slopes = jnp.exp2(-8.0 * (jnp.arange(H, dtype=jnp.int32).astype(jnp.float32) + 1.0) / H)
    positions = jnp.arange(SEQ, dtype=jnp.int32)
    score_scale = 1.0 / math.sqrt(DH)

    def score_block(row_start):
        q_rows = lax.dynamic_slice_in_dim(queries, row_start, QBLK, 0)
        doc_rows = lax.dynamic_slice_in_dim(doc_row, row_start, QBLK, 0)
        row_pos = row_start + jnp.arange(QBLK, dtype=jnp.int32)
        scores = jnp.einsum('qhd,khd->hqk', q_rows, keys_all, precision=highest) * score_scale
        distance = (row_pos[:, None] - positions[None, :]).astype(jnp.float32)
        scores = low_back(scores - slopes[:, None, None] * distance[None])
        allowed = (doc_rows[:, None] == doc_row[None, :]) & (positions[None, :] <= row_pos[:, None])
        scores = jnp.where(allowed[None], scores, -jnp.inf)
        attn_prob = low(jax.nn.softmax(scores, axis=-1))
        return jnp.einsum('hqk,khd->qhd', attn_prob, values, precision=highest)
    starts = (jnp.arange(SEQ // QBLK, dtype=jnp.int32) * QBLK).astype(jnp.int32)
    blocks = lax.map(jax.checkpoint(score_block), starts)
    return blocks.reshape(SEQ, D)

def apply_layer(attn_w, mlp_w, acts, doc_row):
    w_qkv = attn_w[:, :3 * D]
    w_dense = attn_w[:, 3 * D:4 * D]
    gain_one = attn_w[:, 4 * D]
    shift_one = attn_w[:, 4 * D + 1]
    bias_query = attn_w[:, 4 * D + 2]
    bias_value = attn_w[:, 4 * D + 3]
    bias_dense = attn_w[:, 4 * D + 4]
    w_up = mlp_w[:, :FF]
    w_down_t = mlp_w[:, FF:2 * FF]
    gain_two = mlp_w[:, 2 * FF]
    shift_two = mlp_w[:, 2 * FF + 1]
    bias_up = mlp_w[:, 2 * FF + 2:2 * FF + 2 + UPC].T.reshape(FF)
    bias_down = mlp_w[:, 2 * FF + 2 + UPC]
    normed = low(layer_norm(acts, gain_one, shift_one))
    qkv_bias = jnp.concatenate([bias_query, jnp.zeros_like(bias_query), bias_value])
    projected = low(low_back(jnp.dot(normed, w_qkv, precision=highest) + qkv_bias))
    queries = projected[:, :D].reshape(SEQ, H, DH)
    keys_all = projected[:, D:2 * D].reshape(SEQ, H, DH)
    values = projected[:, 2 * D:].reshape(SEQ, H, DH)
    attended = low(low_back(attend(queries, keys_all, values, doc_row)))
    branch = low_back(jnp.dot(attended, w_dense, precision=highest) + bias_dense)
    middle = acts + branch
    normed_two = low(layer_norm(middle, gain_two, shift_two))
    upper = low_back(jnp.dot(normed_two, w_up, precision=highest) + bias_up)
    active = low(gelu_tanh(upper))
    down_out = low_back(jnp.dot(active, w_down_t.T, precision=highest) + bias_down)
    return middle + down_out

def adam_update(weights, first, second, gradient, step_count):
    steps_done = step_count[0].astype(jnp.float32)
    first_new = beta_one * first + (1.0 - beta_one) * gradient
    second_new = beta_two * second + (1.0 - beta_two) * gradient * gradient
    fix_one = 1.0 - jnp.power(beta_one, steps_done)
    fix_two = 1.0 - jnp.power(beta_two, steps_done)
    update = first_new / fix_one / (jnp.sqrt(second_new / fix_two) + adam_eps)
    return (weights - learn_rate * (update + decay_rate * weights), first_new, second_new)

def reference(inputs, cotangent, teacher, document_ids, valid_flags, step_count, attn_params, attn_first, attn_second, mlp_params, mlp_first, mlp_second):

    def forward(attn_p, mlp_p, acts):
        attn_w = low(attn_p)
        mlp_w = low(mlp_p)

        def one_sequence(carried, item_pair):
            return (carried, apply_layer(attn_w, mlp_w, item_pair[0], item_pair[1]))
        _, stacked = lax.scan(one_sequence, jnp.zeros((), jnp.float32), (acts, document_ids))
        return stacked
    acts = inputs.astype(jnp.float32)
    result, pullback = jax.vjp(forward, attn_params, mlp_params, acts)
    valid_float = valid_flags.astype(jnp.float32)
    cot_float = cotangent.astype(jnp.float32)
    deviation = result - teacher.astype(jnp.float32)
    valid_count = jnp.sum(valid_float)
    squared_sum = jnp.sum(valid_float[..., None] * deviation * deviation)
    distill = squared_sum / (valid_count * D)
    result_grad = cot_float + valid_float[..., None] * (TOKENS / valid_count) * deviation
    attn_gradient, mlp_gradient, input_grad = pullback(result_grad)
    vector_gradient = jnp.concatenate([attn_gradient[:, 4 * D:], mlp_gradient[:, 2 * FF:]], axis=1)
    attn_new, attn_first_new, attn_second_new = adam_update(attn_params, attn_first, attn_second, attn_gradient, step_count)
    mlp_new, mlp_first_new, mlp_second_new = adam_update(mlp_params, mlp_first, mlp_second, mlp_gradient, step_count)
    losses = jnp.stack([distill])
    return (result.astype(jnp.bfloat16), losses, input_grad, vector_gradient, attn_new, attn_first_new, attn_second_new, mlp_new, mlp_first_new, mlp_second_new)
```

```python
import math

import jax
import jax.numpy as jnp
from jax import lax
from jax.sharding import PartitionSpec as P

D = 2048
H = 16
DH = 128
FF = 8192
QBLK = 512
UPC = 4

eps_norm = 1e-05
beta_one = 0.9
beta_two = 0.95
adam_eps = 1e-08
decay_rate = 0.1
learn_rate = 0.05
gelu_coef = 0.7978845608028654
BF = jnp.bfloat16
F32 = jnp.float32


def norm_stats(value):
    row_mean = jnp.mean(value, axis=-1, keepdims=True)
    centred = value - row_mean
    variance = jnp.mean(centred * centred, axis=-1, keepdims=True)
    scale = lax.rsqrt(variance + eps_norm)
    return centred * scale, scale


def norm_back(grad, gain, hat, scale):
    e = grad * gain
    return scale * (
        e
        - jnp.mean(e, axis=-1, keepdims=True)
        - hat * jnp.mean(e * hat, axis=-1, keepdims=True)
    )


def gelu_tanh(value):
    return 0.5 * value * (1.0 + jnp.tanh(gelu_coef * (value + 0.044715 * value * value * value)))


def adam_update(weights, first, second, gradient, step_count):
    steps_done = step_count[0].astype(F32)
    first_new = beta_one * first + (1.0 - beta_one) * gradient
    second_new = beta_two * second + (1.0 - beta_two) * gradient * gradient
    fix_one = 1.0 - jnp.power(beta_one, steps_done)
    fix_two = 1.0 - jnp.power(beta_two, steps_done)
    update = first_new / fix_one / (jnp.sqrt(second_new / fix_two) + adam_eps)
    return (weights - learn_rate * (update + decay_rate * weights), first_new, second_new)


def contract_rows(left, right, out=F32):
    return lax.dot_general(
        left, right, (((0,), (0,)), ((), ())), preferred_element_type=F32
    ).astype(out)


def contract_cols(left, right, out=F32):
    return lax.dot_general(
        left, right, (((1,), (1,)), ((), ())), preferred_element_type=F32
    ).astype(out)


def dot(left, right):
    return jnp.dot(left, right, preferred_element_type=F32)


def block_scores(q_rows, key_rows, row_start, slopes, doc_row, score_scale):
    rows_here = q_rows.shape[0]
    keys_here = key_rows.shape[0]
    scores = (
        jnp.einsum("qhd,khd->hqk", q_rows, key_rows, preferred_element_type=F32) * score_scale
    )
    row_pos = row_start + jnp.arange(rows_here, dtype=jnp.int32)
    key_pos = jnp.arange(keys_here, dtype=jnp.int32)
    distance = (row_pos[:, None] - key_pos[None, :]).astype(F32)
    scores = scores - slopes[:, None, None] * distance[None]
    doc_rows = doc_row[row_start : row_start + rows_here]
    allowed = (doc_rows[:, None] == doc_row[None, :]) & (key_pos[None, :] <= row_pos[:, None])
    return jnp.where(allowed[None], scores, -jnp.inf)


def shards(
    inputs,
    cotangent,
    teacher,
    document_ids,
    valid_flags,
    step_count,
    attn_params,
    attn_first,
    attn_second,
    mlp_params,
    mlp_first,
    mlp_second,
):
    tok_rows = inputs.shape[1]
    seq_size = lax.axis_size("seq")
    wsh_size = lax.axis_size("wsh")
    seq_at = lax.axis_index("seq")
    wsh_at = lax.axis_index("wsh")
    own_rows = attn_params.shape[0]
    seq_len = tok_rows * seq_size
    token_total = seq_len * wsh_size
    heads_here = H // seq_size
    head_cols = heads_here * DH
    ff_cols = FF // wsh_size
    score_scale = 1.0 / math.sqrt(DH)
    nblocks = seq_len // QBLK

    own_vectors = jnp.concatenate([attn_params[:, 4 * D :], mlp_params[:, 2 * FF :]], axis=1)
    vectors = lax.all_gather(own_vectors.astype(BF), ("seq", "wsh"), axis=0, tiled=True).astype(F32)
    gain_one, shift_one, bias_query, bias_value, bias_dense = (vectors[:, i] for i in range(5))
    gain_two, shift_two = vectors[:, 5], vectors[:, 6]
    bias_up = vectors[:, 7 : 7 + UPC].T.reshape(FF)
    bias_down = vectors[:, 7 + UPC]

    inputs_all = lax.all_gather(inputs[0], "seq", axis=0, tiled=True)

    qkv_own = attn_params[:, : 3 * D].astype(BF).reshape(own_rows, 3, seq_size, head_cols)
    qkv_cols = lax.all_to_all(
        qkv_own.transpose(2, 0, 1, 3), "seq", split_axis=0, concat_axis=0, tiled=True
    )
    w_qkv = lax.all_gather(qkv_cols, "wsh", axis=1)
    w_qkv = w_qkv.reshape(D, 3 * head_cols)
    w_dense = lax.all_gather(attn_params[:, 3 * D : 4 * D].astype(BF), "wsh", axis=0, tiled=True)

    mlp_own = mlp_params[:, : 2 * FF].astype(BF).reshape(own_rows, 2, wsh_size, ff_cols)
    mlp_cols = lax.all_to_all(
        mlp_own.transpose(2, 0, 1, 3), "wsh", split_axis=0, concat_axis=0, tiled=True
    )
    w_mlp = lax.all_gather(
        mlp_cols.reshape(wsh_size * own_rows, 2 * ff_cols), "seq", axis=0, tiled=True
    )
    w_up = w_mlp[:, :ff_cols]
    w_down_t = w_mlp[:, ff_cols:]

    valid_float = valid_flags[0].astype(F32)
    valid_count = lax.psum(jnp.sum(valid_float), ("seq", "wsh"))

    normed_low = (norm_stats(inputs_all.astype(F32))[0] * gain_one + shift_one).astype(BF)
    acts = inputs[0].astype(F32)
    hat_one, scale_one = norm_stats(acts)
    bias_q = lax.dynamic_slice(bias_query, (seq_at * head_cols,), (head_cols,))
    bias_v = lax.dynamic_slice(bias_value, (seq_at * head_cols,), (head_cols,))
    qkv_bias = jnp.concatenate([bias_q, jnp.zeros_like(bias_q), bias_v])
    projected = (dot(normed_low, w_qkv) + qkv_bias).astype(BF)
    arrived = projected.reshape(seq_len, 3, heads_here, DH)
    queries = arrived[:, 0]
    keys_all = arrived[:, 1]
    values = arrived[:, 2]
    head_ids = seq_at * heads_here + jnp.arange(heads_here, dtype=jnp.int32)
    slopes = jnp.exp2(-8.0 * (head_ids.astype(F32) + 1.0) / H)
    doc_row = document_ids[0]
    out_blocks = []
    log_blocks = []
    for block_index in range(nblocks):
        row_start = block_index * QBLK
        scores = block_scores(
            queries[row_start : row_start + QBLK], keys_all, row_start, slopes, doc_row, score_scale
        )
        row_top = jnp.max(scores, axis=-1, keepdims=True)
        exp_scores = jnp.exp(scores - row_top)
        row_total = jnp.sum(exp_scores, axis=-1, keepdims=True)
        prob_low = (exp_scores / row_total).astype(BF)
        log_blocks.append((row_top + jnp.log(row_total))[..., 0])
        block_out = jnp.einsum("hqk,khd->qhd", prob_low, values, preferred_element_type=F32)
        out_blocks.append(block_out.astype(BF))
    attended = jnp.concatenate(out_blocks, axis=0).reshape(seq_len, head_cols)
    log_total = jnp.concatenate(log_blocks, axis=1)
    dense_out = lax.psum_scatter(
        dot(attended, w_dense).astype(BF), "seq", scatter_dimension=0, tiled=True
    )
    middle = acts + dense_out.astype(F32) + bias_dense

    hat_two, scale_two = norm_stats(middle)
    normed_two_low = (hat_two * gain_two + shift_two).astype(BF)
    normed_two_all = lax.all_gather(normed_two_low, "wsh", axis=0, tiled=True)
    bias_up_here = lax.dynamic_slice(bias_up, (wsh_at * ff_cols,), (ff_cols,))
    upper = dot(normed_two_all, w_up) + bias_up_here
    active, gelu_back = jax.vjp(gelu_tanh, upper)
    active_low = active.astype(BF)
    down_out = lax.psum_scatter(
        contract_cols(active_low, w_down_t, BF), "wsh", scatter_dimension=0, tiled=True
    )
    result = middle + down_out.astype(F32) + bias_down

    cot_float = cotangent[0].astype(F32)
    deviation = result - teacher[0].astype(F32)
    squared_sum = lax.psum(jnp.sum(valid_float[:, None] * deviation * deviation), ("seq", "wsh"))
    losses = jnp.stack([squared_sum / (valid_count * D)])
    result_grad = cot_float + valid_float[:, None] * (token_total / valid_count) * deviation
    down_grad = result_grad.astype(BF)

    down_grad_all = lax.all_gather(down_grad, "wsh", axis=0, tiled=True)
    (upper_grad,) = gelu_back(dot(down_grad_all, w_down_t))
    upper_low = upper_grad.astype(BF)
    normed_two_grad = lax.psum_scatter(
        contract_cols(upper_low, w_up, BF), "wsh", scatter_dimension=0, tiled=True
    ).astype(F32)
    up_part = contract_rows(normed_two_all, upper_low, BF)
    down_part = contract_rows(down_grad_all, active_low, BF)
    mlp_rows = lax.psum_scatter(
        jnp.concatenate([up_part, down_part], axis=1), "seq", scatter_dimension=0, tiled=True
    )
    mlp_gradient = lax.all_to_all(
        mlp_rows.reshape(wsh_size, own_rows, 2, ff_cols),
        "wsh",
        split_axis=0,
        concat_axis=0,
        tiled=True,
    )
    mlp_gradient = mlp_gradient.transpose(1, 2, 0, 3).reshape(own_rows, 2 * FF).astype(F32)
    middle_grad = result_grad + norm_back(normed_two_grad, gain_two, hat_two, scale_two)

    dense_grad = middle_grad.astype(BF)
    dense_grad_all = lax.all_gather(dense_grad, "seq", axis=0, tiled=True)
    out_grad = contract_cols(dense_grad_all, w_dense, BF).reshape(seq_len, heads_here, DH)
    dense_part = contract_rows(attended, dense_grad_all, BF)
    key_grad = jnp.zeros((seq_len, heads_here, DH), F32)
    value_grad = jnp.zeros((seq_len, heads_here, DH), F32)
    query_blocks = []
    for block_index in range(nblocks):
        row_start = block_index * QBLK
        q_rows = queries[row_start : row_start + QBLK]
        grad_rows = out_grad[row_start : row_start + QBLK]
        scores = block_scores(q_rows, keys_all, row_start, slopes, doc_row, score_scale)
        prob = jnp.exp(scores - log_total[:, row_start : row_start + QBLK, None])
        prob_low = prob.astype(BF)
        prob_grad = jnp.einsum("qhd,khd->hqk", grad_rows, values, preferred_element_type=F32)
        row_delta = jnp.sum(prob * prob_grad, axis=-1, keepdims=True)
        score_grad = (prob * (prob_grad - row_delta)).astype(BF)
        query_blocks.append(
            jnp.einsum("hqk,khd->qhd", score_grad, keys_all, preferred_element_type=F32)
            * score_scale
        )
        key_grad = key_grad + (
            jnp.einsum("hqk,qhd->khd", score_grad, q_rows, preferred_element_type=F32)
            * score_scale
        )
        value_grad = value_grad + jnp.einsum(
            "hqk,qhd->khd", prob_low, grad_rows, preferred_element_type=F32
        )
    query_grad = jnp.concatenate(query_blocks, axis=0)
    projected_grad = (
        jnp.stack([query_grad, key_grad, value_grad], axis=1)
        .astype(BF)
        .reshape(seq_len, 3 * head_cols)
    )
    normed_grad = lax.psum_scatter(
        contract_cols(projected_grad, w_qkv, BF), "seq", scatter_dimension=0, tiled=True
    ).astype(F32)
    input_grad = middle_grad + norm_back(normed_grad, gain_one, hat_one, scale_one)
    qkv_part = contract_rows(normed_low, projected_grad, BF)
    qkv_rows = lax.psum_scatter(
        qkv_part.reshape(seq_size, wsh_size, own_rows, 3 * head_cols),
        "wsh",
        scatter_dimension=1,
        tiled=True,
    ).reshape(seq_size, own_rows, 3, head_cols)
    qkv_gradient = lax.all_to_all(qkv_rows, "seq", split_axis=0, concat_axis=0, tiled=True)
    qkv_gradient = qkv_gradient.transpose(1, 2, 0, 3).reshape(own_rows, 3 * D)
    dense_gradient = lax.psum_scatter(dense_part, "wsh", scatter_dimension=0, tiled=True)
    attn_gradient = jnp.concatenate([qkv_gradient, dense_gradient], axis=1).astype(F32)

    zeros = jnp.zeros((D,), F32)
    qkv_sums = jnp.sum(projected_grad, axis=0, dtype=F32)
    query_sums = lax.dynamic_update_slice(zeros, qkv_sums[:head_cols], (seq_at * head_cols,))
    value_sums = lax.dynamic_update_slice(zeros, qkv_sums[2 * head_cols :], (seq_at * head_cols,))
    up_sums = lax.dynamic_update_slice(
        jnp.zeros((FF,), F32), jnp.sum(upper_low, axis=0, dtype=F32), (wsh_at * ff_cols,)
    )
    vector_part = jnp.concatenate(
        [
            jnp.stack(
                [
                    jnp.sum(normed_grad * hat_one, axis=0),
                    jnp.sum(normed_grad, axis=0),
                    query_sums,
                    value_sums,
                    jnp.sum(dense_grad, axis=0, dtype=F32),
                    jnp.sum(normed_two_grad * hat_two, axis=0),
                    jnp.sum(normed_two_grad, axis=0),
                ],
                axis=1,
            ),
            up_sums.reshape(UPC, D).T,
            jnp.sum(down_grad, axis=0, dtype=F32)[:, None],
        ],
        axis=1,
    )
    vector_gradient = lax.psum_scatter(
        vector_part, ("seq", "wsh"), scatter_dimension=0, tiled=True
    )
    attn_gradient = jnp.concatenate([attn_gradient, vector_gradient[:, :5]], axis=1)
    mlp_gradient = jnp.concatenate([mlp_gradient, vector_gradient[:, 5:]], axis=1)
    attn_new, attn_first_new, attn_second_new = adam_update(
        attn_params, attn_first, attn_second, attn_gradient, step_count
    )
    mlp_new, mlp_first_new, mlp_second_new = adam_update(
        mlp_params, mlp_first, mlp_second, mlp_gradient, step_count
    )
    return (
        result.astype(BF)[None],
        losses,
        input_grad[None],
        vector_gradient,
        attn_new,
        attn_first_new,
        attn_second_new,
        mlp_new,
        mlp_first_new,
        mlp_second_new,
    )


def solution(mesh):
    rows = P(("seq", "wsh"), None)
    tokens = P("wsh", "seq", None)
    return jax.shard_map(
        shards,
        mesh=mesh,
        in_specs=(tokens, tokens, tokens, P("wsh", None), P("wsh", "seq"), P()) + (rows,) * 6,
        out_specs=(tokens, P(), tokens) + (rows,) * 7,
        check_vma=False,
    )
```

```python
import functools
import math

import jax
import jax.numpy as jnp
from jax import lax
from jax.experimental import pallas as pl
from jax.experimental.pallas import tpu as pltpu
from jax.sharding import PartitionSpec as P

D = 2048
H = 16
DH = 128
FF = 8192
QBLK = 512
UPC = 4

eps_norm = 1e-05
beta_one = 0.9
beta_two = 0.95
adam_eps = 1e-08
decay_rate = 0.1
learn_rate = 0.05
gelu_coef = 0.7978845608028654
BF = jnp.bfloat16
F32 = jnp.float32


def norm_stats(value):
    row_mean = jnp.mean(value, axis=-1, keepdims=True)
    centred = value - row_mean
    variance = jnp.mean(centred * centred, axis=-1, keepdims=True)
    scale = lax.rsqrt(variance + eps_norm)
    return centred * scale, scale


def norm_back(grad, gain, hat, scale):
    e = grad * gain
    return scale * (
        e
        - jnp.mean(e, axis=-1, keepdims=True)
        - hat * jnp.mean(e * hat, axis=-1, keepdims=True)
    )


def gelu_tanh(value):
    return 0.5 * value * (1.0 + jnp.tanh(gelu_coef * (value + 0.044715 * value * value * value)))


def adam_update(weights, first, second, gradient, step_count):
    steps_done = step_count[0].astype(F32)
    first_new = beta_one * first + (1.0 - beta_one) * gradient
    second_new = beta_two * second + (1.0 - beta_two) * gradient * gradient
    fix_one = 1.0 - jnp.power(beta_one, steps_done)
    fix_two = 1.0 - jnp.power(beta_two, steps_done)
    update = first_new / fix_one / (jnp.sqrt(second_new / fix_two) + adam_eps)
    return (weights - learn_rate * (update + decay_rate * weights), first_new, second_new)


def contract_rows(left, right, out=F32):
    return lax.dot_general(
        left, right, (((0,), (0,)), ((), ())), preferred_element_type=F32
    ).astype(out)


def contract_cols(left, right, out=F32):
    return lax.dot_general(
        left, right, (((1,), (1,)), ((), ())), preferred_element_type=F32
    ).astype(out)


def dot(left, right):
    return jnp.dot(left, right, preferred_element_type=F32)


def block_scores(q_rows, key_rows, row_pos, key_pos, row_docs, key_docs, slopes, score_scale):
    scores = (
        jnp.einsum("qhd,khd->hqk", q_rows, key_rows, preferred_element_type=F32) * score_scale
    )
    distance = (row_pos[:, None] - key_pos[None, :]).astype(F32)
    scores = scores - slopes[:, None, None] * distance[None]
    allowed = (row_docs[:, None] == key_docs[None, :]) & (key_pos[None, :] <= row_pos[:, None])
    return jnp.where(allowed[None], scores, -jnp.inf)


def exchange_body(seq_size, wsh_size, spread, block_ref, out_ref, send_sems, recv_sems, own_sem):
    total = seq_size * wsh_size
    me = lax.axis_index("seq") * wsh_size + lax.axis_index("wsh")
    barrier = pltpu.get_barrier_semaphore()

    def place(index):
        return (index // wsh_size, index % wsh_size)

    def greet(step, carry):
        pl.semaphore_signal(
            barrier, inc=1, device_id=place((me + step) % total), device_id_type=pl.DeviceIdType.MESH
        )
        return carry

    lax.fori_loop(1, total, greet, 0)
    pl.semaphore_wait(barrier, total - 1)

    def copy(step):
        peer = (me + step) % total
        return pltpu.make_async_remote_copy(
            src_ref=block_ref.at[peer if spread else 0],
            dst_ref=out_ref.at[me],
            send_sem=send_sems.at[step],
            recv_sem=recv_sems.at[step],
            device_id=place(peer),
            device_id_type=pl.DeviceIdType.MESH,
        )

    own = pltpu.make_async_copy(block_ref.at[me if spread else 0], out_ref.at[me], own_sem)
    own.start()

    def start(step, carry):
        copy(step).start()
        return carry

    def finish(step, carry):
        copy(step).wait()
        return carry

    lax.fori_loop(1, total, start, 0)
    lax.fori_loop(1, total, finish, 0)
    own.wait()


def exchange_small(blocks, spread, seq_size, wsh_size, number):
    total = seq_size * wsh_size
    vmem = pl.BlockSpec(memory_space=pltpu.VMEM)
    return pl.pallas_call(
        functools.partial(exchange_body, seq_size, wsh_size, spread),
        out_shape=jax.ShapeDtypeStruct((total,) + blocks.shape[1:], blocks.dtype),
        in_specs=[vmem],
        out_specs=vmem,
        scratch_shapes=[
            pltpu.SemaphoreType.DMA((total,)),
            pltpu.SemaphoreType.DMA((total,)),
            pltpu.SemaphoreType.DMA,
        ],
        compiler_params=pltpu.CompilerParams(collective_id=number, has_side_effects=True),
    )(blocks)


def pack_tile(values):
    flat = values.reshape(values.shape[0], -1)
    width = -(-flat.shape[1] // 1024) * 1024
    flat = jnp.pad(flat, ((0, 0), (0, width - flat.shape[1])))
    return flat.reshape(values.shape[0], width // 128, 128)


def unpack_tile(tiles, shape):
    count = math.prod(shape)
    return tiles.reshape(tiles.shape[0], -1)[:, :count].reshape((tiles.shape[0],) + shape)


def ring_gather(rows, axis, size):
    half = rows.shape[0] // 2
    upper, lower = rows[:half], rows[half:]
    steps = [(upper, lower)]
    for _ in range(1, size):
        upper = lax.ppermute(upper, axis, [(i, (i + 1) % size) for i in range(size)])
        lower = lax.ppermute(lower, axis, [(i, (i - 1) % size) for i in range(size)])
        steps.append((upper, lower))
    return steps


def ring_scatter(steps, axis, size):
    upper, lower = steps[1]
    for k in range(2, size + 1):
        upper = lax.ppermute(upper, axis, [(i, (i + 1) % size) for i in range(size)])
        lower = lax.ppermute(lower, axis, [(i, (i - 1) % size) for i in range(size)])
        upper = upper.astype(F32) + steps[k % size][0].astype(F32)
        lower = lower.astype(F32) + steps[k % size][1].astype(F32)
        if k < size:
            upper, lower = upper.astype(BF), lower.astype(BF)
    return jnp.concatenate([upper, lower], axis=0)


def swap(value, mask, axis, size):
    return lax.ppermute(value, axis, [(i, i ^ mask) for i in range(size)])


def plane_gather(rows, axis, size):
    if size != 8:
        parts = lax.all_gather(rows, axis, axis=0)
        return [parts[i] for i in range(size)]
    half = rows.shape[0] // 2
    across = swap(rows, 2, axis, size)
    along = swap(rows, 4, axis, size)
    corner = jnp.concatenate(
        [swap(across[:half], 4, axis, size), swap(along[half:], 2, axis, size)], axis=0
    )
    blocks = []
    for block in (rows, across, along, corner):
        blocks += [block, swap(block, 1, axis, size)]
    return blocks


def plane_scatter(blocks, axis, size):
    if size != 8:
        return lax.psum_scatter(
            jnp.stack(blocks), axis, scatter_dimension=0, tiled=False
        ).astype(F32)
    half = blocks[0].shape[0] // 2

    def add(left, right):
        return (left.astype(F32) + right.astype(F32)).astype(BF)

    corner = add(blocks[6], swap(blocks[7], 1, axis, size))
    across = add(blocks[2], swap(blocks[3], 1, axis, size))
    along = add(blocks[4], swap(blocks[5], 1, axis, size))
    own = add(blocks[0], swap(blocks[1], 1, axis, size))
    along_upper = add(along[:half], swap(corner[:half], 2, axis, size))
    across_lower = add(across[half:], swap(corner[half:], 4, axis, size))
    across_sum = jnp.concatenate([across[:half], across_lower], axis=0)
    along_sum = jnp.concatenate([along_upper, along[half:]], axis=0)
    return (
        own.astype(F32)
        + swap(across_sum, 2, axis, size).astype(F32)
        + swap(along_sum, 4, axis, size).astype(F32)
    )


def shards(
    inputs,
    cotangent,
    teacher,
    document_ids,
    valid_flags,
    step_count,
    attn_params,
    attn_first,
    attn_second,
    mlp_params,
    mlp_first,
    mlp_second,
):
    tok_rows = inputs.shape[1]
    seq_size = lax.axis_size("seq")
    wsh_size = lax.axis_size("wsh")
    seq_at = lax.axis_index("seq")
    wsh_at = lax.axis_index("wsh")
    own_rows = attn_params.shape[0]
    seq_len = tok_rows * seq_size
    token_total = seq_len * wsh_size
    heads_here = H // seq_size
    head_cols = heads_here * DH
    ff_cols = FF // wsh_size
    score_scale = 1.0 / math.sqrt(DH)
    nblocks = seq_len // QBLK

    input_steps = ring_gather(inputs[0], "seq", seq_size)
    half_rows = tok_rows // 2
    group = QBLK // tok_rows

    def grouped(steps, index):
        parts = []
        for pair in steps[index * group : (index + 1) * group]:
            parts += list(pair)
        return jnp.concatenate(parts, axis=0)

    def ungrouped(blocks):
        steps = []
        for block in blocks:
            for k in range(group):
                base = k * tok_rows
                steps.append(
                    (block[base : base + half_rows], block[base + half_rows : base + tok_rows])
                )
        return steps

    starts = []
    for k in range(seq_size):
        starts.append(
            (
                ((seq_at - k) % seq_size) * tok_rows,
                ((seq_at + k) % seq_size) * tok_rows + half_rows,
            )
        )
    ramp = jnp.arange(half_rows, dtype=jnp.int32)
    row_pos = [grouped([(a + ramp, b + ramp) for a, b in starts], g) for g in range(nblocks)]
    doc_row = document_ids[0]
    doc_steps = [
        tuple(lax.dynamic_slice(doc_row, (at,), (half_rows,)) for at in pair) for pair in starts
    ]
    row_docs = [grouped(doc_steps, g) for g in range(nblocks)]
    key_pos = jnp.concatenate(row_pos)
    key_docs = jnp.concatenate(row_docs)

    valid_float = valid_flags[0].astype(F32)
    own_vectors = jnp.concatenate([attn_params[:, 4 * D :], mlp_params[:, 2 * FF :]], axis=1)
    own_vectors = own_vectors.astype(BF).astype(F32)
    count_column = jnp.zeros((own_rows, 1), F32).at[0, 0].set(jnp.sum(valid_float))
    arrived_vectors = exchange_small(
        pack_tile(jnp.concatenate([own_vectors, count_column], axis=1)[None]),
        False,
        seq_size,
        wsh_size,
        0,
    )
    vectors = unpack_tile(arrived_vectors, (own_rows, 13)).reshape(D, 13)
    valid_count = jnp.sum(vectors[:, 12])
    gain_one, shift_one, bias_query, bias_value, bias_dense = (vectors[:, i] for i in range(5))
    gain_two, shift_two = vectors[:, 5], vectors[:, 6]
    bias_up = vectors[:, 7 : 7 + UPC].T.reshape(FF)
    bias_down = vectors[:, 7 + UPC]

    attn_low = attn_params[:, : 4 * D].astype(BF)
    qkv_own = jnp.stack(
        [
            jnp.concatenate(
                [
                    attn_low[:, part * D + s * head_cols : part * D + (s + 1) * head_cols]
                    for part in range(3)
                ],
                axis=1,
            )
            for s in range(seq_size)
        ]
    )
    qkv_cols = lax.all_to_all(qkv_own, "seq", split_axis=0, concat_axis=0, tiled=True)
    w_qkv = lax.all_gather(qkv_cols, "wsh", axis=1)
    w_qkv = w_qkv.reshape(D, 3 * head_cols)
    w_dense = lax.all_gather(attn_low[:, 3 * D :], "wsh", axis=0, tiled=True)

    mlp_low = mlp_params[:, : 2 * FF].astype(BF)
    mlp_own = jnp.stack(
        [
            jnp.concatenate(
                [mlp_low[:, part * FF + w * ff_cols : part * FF + (w + 1) * ff_cols] for part in range(2)],
                axis=1,
            )
            for w in range(wsh_size)
        ]
    )
    mlp_cols = lax.all_to_all(mlp_own, "wsh", split_axis=0, concat_axis=0, tiled=True)
    mlp_cols = mlp_cols.reshape(wsh_size * own_rows, 2 * ff_cols)
    w_up = lax.all_gather(mlp_cols[:, :ff_cols], "seq", axis=0, tiled=True)
    w_down_t = lax.all_gather(mlp_cols[:, ff_cols:], "seq", axis=0, tiled=True)

    acts = inputs[0].astype(F32)
    hat_one, scale_one = norm_stats(acts)
    bias_q = lax.dynamic_slice(bias_query, (seq_at * head_cols,), (head_cols,))
    bias_v = lax.dynamic_slice(bias_value, (seq_at * head_cols,), (head_cols,))
    qkv_bias = jnp.concatenate([bias_q, jnp.zeros_like(bias_q), bias_v])
    normed_blocks = []
    projected_blocks = []
    for g in range(nblocks):
        rows = grouped(input_steps, g).astype(F32)
        normed_blocks.append((norm_stats(rows)[0] * gain_one + shift_one).astype(BF))
        projected_blocks.append(
            (dot(normed_blocks[g], w_qkv) + qkv_bias).astype(BF).reshape(QBLK, 3, heads_here, DH)
        )
    queries = [block[:, 0] for block in projected_blocks]
    keys_all = jnp.concatenate([block[:, 1] for block in projected_blocks], axis=0)
    values = jnp.concatenate([block[:, 2] for block in projected_blocks], axis=0)
    head_ids = seq_at * heads_here + jnp.arange(heads_here, dtype=jnp.int32)
    slopes = jnp.exp2(-8.0 * (head_ids.astype(F32) + 1.0) / H)
    attended_blocks = []
    log_blocks = []
    dense_blocks = []
    for g in range(nblocks):
        scores = block_scores(
            queries[g], keys_all, row_pos[g], key_pos, row_docs[g], key_docs, slopes, score_scale
        )
        row_top = jnp.max(scores, axis=-1, keepdims=True)
        exp_scores = jnp.exp(scores - row_top)
        row_total = jnp.sum(exp_scores, axis=-1, keepdims=True)
        prob_low = (exp_scores / row_total).astype(BF)
        log_blocks.append(row_top + jnp.log(row_total))
        block_out = jnp.einsum("hqk,khd->qhd", prob_low, values, preferred_element_type=F32)
        attended_blocks.append(block_out.astype(BF).reshape(QBLK, head_cols))
        dense_blocks.append(dot(attended_blocks[g], w_dense).astype(BF))
    dense_out = ring_scatter(ungrouped(dense_blocks), "seq", seq_size)
    middle = acts + dense_out + bias_dense

    hat_two, scale_two = norm_stats(middle)
    normed_two_low = (hat_two * gain_two + shift_two).astype(BF)
    normed_two_parts = plane_gather(normed_two_low, "wsh", wsh_size)
    bias_up_here = lax.dynamic_slice(bias_up, (wsh_at * ff_cols,), (ff_cols,))
    upper_parts = [dot(part, w_up) + bias_up_here for part in normed_two_parts]
    active_parts = [gelu_tanh(part).astype(BF) for part in upper_parts]
    down_out = plane_scatter(
        [contract_cols(part, w_down_t, BF) for part in active_parts], "wsh", wsh_size
    )
    result = middle + down_out + bias_down

    cot_float = cotangent[0].astype(F32)
    deviation = result - teacher[0].astype(F32)
    squared_part = jnp.sum(valid_float[:, None] * deviation * deviation)
    result_grad = cot_float + valid_float[:, None] * (token_total / valid_count) * deviation
    down_grad = result_grad.astype(BF)

    down_grad_parts = plane_gather(down_grad, "wsh", wsh_size)
    upper_low_parts = []
    for grad_part, upper_part in zip(down_grad_parts, upper_parts):
        gelu_back = jax.vjp(gelu_tanh, upper_part)[1]
        (upper_grad,) = gelu_back(dot(grad_part, w_down_t))
        upper_low_parts.append(upper_grad.astype(BF))
    normed_two_grad = plane_scatter(
        [contract_cols(part, w_up, BF) for part in upper_low_parts], "wsh", wsh_size
    )
    upper_low = jnp.concatenate(upper_low_parts, axis=0)
    down_part = contract_rows(
        jnp.concatenate(down_grad_parts, axis=0), jnp.concatenate(active_parts, axis=0), BF
    )
    up_part = contract_rows(jnp.concatenate(normed_two_parts, axis=0), upper_low, BF)

    def mlp_rows(part):
        rows = lax.psum_scatter(part, "seq", scatter_dimension=0, tiled=True)
        rows = lax.all_to_all(
            rows.reshape(wsh_size, own_rows, ff_cols), "wsh", split_axis=0, concat_axis=0, tiled=True
        )
        return [rows[w] for w in range(wsh_size)]

    down_rows = mlp_rows(down_part)
    up_rows = mlp_rows(up_part)
    mlp_gradient = jnp.concatenate(up_rows + down_rows, axis=1).astype(F32)
    middle_grad = result_grad + norm_back(normed_two_grad, gain_two, hat_two, scale_two)

    dense_grad = middle_grad.astype(BF)
    grad_steps = ring_gather(dense_grad, "seq", seq_size)
    key_grad = jnp.zeros((seq_len, heads_here, DH), F32)
    value_grad = jnp.zeros((seq_len, heads_here, DH), F32)
    grad_blocks = []
    query_blocks = []
    for g in range(nblocks):
        grad_blocks.append(grouped(grad_steps, g))
        q_rows = queries[g]
        grad_rows = contract_cols(grad_blocks[g], w_dense, BF).reshape(QBLK, heads_here, DH)
        scores = block_scores(
            q_rows, keys_all, row_pos[g], key_pos, row_docs[g], key_docs, slopes, score_scale
        )
        prob = jnp.exp(scores - log_blocks[g])
        prob_low = prob.astype(BF)
        prob_grad = jnp.einsum("qhd,khd->hqk", grad_rows, values, preferred_element_type=F32)
        row_delta = jnp.sum(prob * prob_grad, axis=-1, keepdims=True)
        score_grad = (prob * (prob_grad - row_delta)).astype(BF)
        query_blocks.append(
            jnp.einsum("hqk,khd->qhd", score_grad, keys_all, preferred_element_type=F32)
            * score_scale
        )
        key_grad = key_grad + (
            jnp.einsum("hqk,qhd->khd", score_grad, q_rows, preferred_element_type=F32)
            * score_scale
        )
        value_grad = value_grad + jnp.einsum(
            "hqk,qhd->khd", prob_low, grad_rows, preferred_element_type=F32
        )
    query_grad = jnp.concatenate(query_blocks, axis=0)
    projected_grad = jnp.concatenate(
        [
            part.astype(BF).reshape(seq_len, head_cols)
            for part in (query_grad, key_grad, value_grad)
        ],
        axis=1,
    )
    normed_blocks_grad = [
        contract_cols(projected_grad[g * QBLK : (g + 1) * QBLK], w_qkv, BF) for g in range(nblocks)
    ]
    normed_grad = ring_scatter(ungrouped(normed_blocks_grad), "seq", seq_size)
    input_grad = middle_grad + norm_back(normed_grad, gain_one, hat_one, scale_one)
    dense_part = contract_rows(
        jnp.concatenate(attended_blocks, axis=0), jnp.concatenate(grad_blocks, axis=0), BF
    )
    qkv_part = contract_rows(jnp.concatenate(normed_blocks, axis=0), projected_grad, BF)
    qkv_rows = lax.psum_scatter(
        qkv_part.reshape(seq_size, wsh_size, own_rows, 3 * head_cols),
        "wsh",
        scatter_dimension=1,
        tiled=True,
    ).reshape(seq_size, own_rows, 3 * head_cols)
    qkv_gradient = lax.all_to_all(qkv_rows, "seq", split_axis=0, concat_axis=0, tiled=True)
    qkv_gradient = [
        qkv_gradient[s, :, part * head_cols : (part + 1) * head_cols]
        for part in range(3)
        for s in range(seq_size)
    ]
    dense_gradient = lax.psum_scatter(dense_part, "wsh", scatter_dimension=0, tiled=True)
    attn_gradient = jnp.concatenate(qkv_gradient + [dense_gradient], axis=1).astype(F32)

    zeros = jnp.zeros((D,), F32)
    qkv_sums = jnp.sum(projected_grad, axis=0, dtype=F32)
    query_sums = lax.dynamic_update_slice(zeros, qkv_sums[:head_cols], (seq_at * head_cols,))
    value_sums = lax.dynamic_update_slice(zeros, qkv_sums[2 * head_cols :], (seq_at * head_cols,))
    up_sums = lax.dynamic_update_slice(
        jnp.zeros((FF,), F32), jnp.sum(upper_low, axis=0, dtype=F32), (wsh_at * ff_cols,)
    )
    vector_part = jnp.concatenate(
        [
            jnp.stack(
                [
                    jnp.sum(normed_grad * hat_one, axis=0),
                    jnp.sum(normed_grad, axis=0),
                    query_sums,
                    value_sums,
                    jnp.sum(dense_grad, axis=0, dtype=F32),
                    jnp.sum(normed_two_grad * hat_two, axis=0),
                    jnp.sum(normed_two_grad, axis=0),
                ],
                axis=1,
            ),
            up_sums.reshape(UPC, D).T,
            jnp.sum(down_grad, axis=0, dtype=F32)[:, None],
            jnp.full((D, 1), squared_part, F32),
        ],
        axis=1,
    )
    arrived_parts = exchange_small(
        pack_tile(vector_part.reshape(seq_size * wsh_size, own_rows, 13)),
        True,
        seq_size,
        wsh_size,
        1,
    )
    vector_sums = unpack_tile(jnp.sum(arrived_parts, axis=0)[None], (own_rows, 13))[0]
    vector_gradient = vector_sums[:, :12]
    losses = jnp.stack([vector_sums[0, 12] / (valid_count * D)])
    attn_gradient = jnp.concatenate([attn_gradient, vector_gradient[:, :5]], axis=1)
    mlp_gradient = jnp.concatenate([mlp_gradient, vector_gradient[:, 5:]], axis=1)
    attn_new, attn_first_new, attn_second_new = adam_update(
        attn_params, attn_first, attn_second, attn_gradient, step_count
    )
    mlp_new, mlp_first_new, mlp_second_new = adam_update(
        mlp_params, mlp_first, mlp_second, mlp_gradient, step_count
    )
    return (
        result.astype(BF)[None],
        losses,
        input_grad[None],
        vector_gradient,
        attn_new,
        attn_first_new,
        attn_second_new,
        mlp_new,
        mlp_first_new,
        mlp_second_new,
    )


def solution(mesh):
    rows = P(("seq", "wsh"), None)
    tokens = P("wsh", "seq", None)
    return jax.shard_map(
        shards,
        mesh=mesh,
        in_specs=(tokens, tokens, tokens, P("wsh", None), P("wsh", "seq"), P()) + (rows,) * 6,
        out_specs=(tokens, P(), tokens) + (rows,) * 7,
        check_vma=False,
    )
```
